128 devices in a mesh: dp: 32 (over y, z, core), rep: 4 (over x).
Axes of the slice: x: 4, y: 4, z: 4, core: 2. Of those that a mesh axis runs over, the one named last changes fastest.
Arguments:
- queries: bfloat16 [8192, 768], P(('dp', 'rep')), may hold values from -60 to 60
- bank: bfloat16 [256, 4096, 768], P('dp', 'rep'), may hold values from -0.21875 to 0.21875
- labels: int32 [256, 4096], P('dp', 'rep'), may hold values from 0 to 127
- probes: int32 [8192, 8], P(('dp', 'rep')), may hold values from 0 to 255, all different within a row; in each aligned block of 64 rows (0 to 63, 64 to 127, ...) at most 4 rows name the same one
Outputs:
- votes: float32 [8192, 128], P(('dp', 'rep'))
The draws below stay inside these ranges and needn't reach their ends.
Inputs may be any that keep to these rules, and one draw needn't show every extreme that they name: `probes`: each row names 8 different clusters; among the rows of one device no cluster is named more than 4 times.
All inputs are finite; a program needn't handle non-finite values.
Results may differ from the reference program's by a relative error of at most 0.0017.
Values may be sent and summed in bfloat16 or wider, within the bound.
No kernel may reach another device: no remote copies, remote signals or barrier semaphores. Data moves between devices by JAX's collectives and lax.ppermute only.
A program may use at most 192 MiB of HBM per device.

```python
import math
import jax
import jax.numpy as jnp
import numpy as np
from jax import lax

D = 768
CLASSES = 128
P_SIZE = 8
R = 4096
Q_DEV = 64
CLUSTERS = 256
QUERIES = 8192
CAP = 4
N_DP = 32
N_REP = 4


def draw_queries(key, part):
    first_key = jax.random.fold_in(jax.random.fold_in(key, 11), 0)
    values = jnp.clip(jax.random.normal(first_key, (QUERIES, D), jnp.float32), -6.0, 6.0)
    return values.astype(jnp.bfloat16)


def touch_ends(values, key, least, top_value):
    longest = values.shape.index(max(values.shape))
    spots = []
    for shift in (0, 1):
        where = [jax.random.randint(jax.random.fold_in(key, axis), (), 0, length) for axis, length in enumerate(values.shape)]
        where[longest] = (where[longest] + shift) % values.shape[longest]
        spots.append(tuple(where))
    return values.at[spots[0]].set(least).at[spots[1]].set(top_value)


def shard_levels(key, shape, shards, low, high):
    def one(axis_at, blocks):
        steps = jax.random.uniform(jax.random.fold_in(jax.random.fold_in(key, 6), axis_at), (blocks,), jnp.float32, low / len(shards), high / len(shards))
        return jnp.repeat(jnp.exp(steps), shape[axis_at] // blocks).reshape((-1,) + (1,) * (len(shape) - axis_at - 1))

    factor_of = one(*shards[0])
    for cut in shards[1:]:
        factor_of = factor_of * one(*cut)
    return factor_of


def routed_block(stream_key, own, number, rows, number_of, top, reach, slope):
    ranking = jax.random.permutation(stream_key, number_of)
    heavy_load, common = portions_of(number_of, rows * top, reach, slope, True), portions_of(number_of, rows * top, reach, slope, False)
    places = jnp.arange(number_of)

    def named(sizes, turn):
        used = int((sizes > 0).sum())
        fixed = max(1, used // 4)
        passed = fixed + (places - fixed + turn * (used - fixed)) % max(1, number_of - fixed)
        return jnp.zeros((number_of,), jnp.int32).at[ranking[jnp.where(places < fixed, places, passed)]].set(jnp.asarray(sizes, jnp.int32))

    sizes = jnp.where(number % 4 == 0, named(heavy_load, number // 4), named(common, number - number // 4 - 1))
    mixed = jax.random.permutation(jax.random.fold_in(own, 3), number_of)
    source_of, taker = mixed[0:number_of // 2 * 2:2], mixed[1:number_of // 2 * 2:2]
    slack = jnp.minimum(sizes[source_of] - 1, reach - sizes[taker]) // 2
    slack = jnp.where((source_of == ranking[0]) | (taker == ranking[0]) | (sizes[taker] == 0), 0, jnp.maximum(slack, 0))
    passed = jax.random.randint(jax.random.fold_in(own, 4), (number_of // 2,), 0, 1 << 20) % (slack + 1)
    sizes = sizes.at[source_of].add(-passed).at[taker].add(passed)
    members = jnp.searchsorted(jnp.cumsum(sizes), jnp.arange(rows * top), side="right").astype(jnp.int32)
    grid = members.reshape(top, rows).T
    grid = grid[jax.random.permutation(jax.random.fold_in(own, 1), rows)]
    turn = jax.random.randint(jax.random.fold_in(own, 2), (rows, 1), 0, top)
    return jnp.take_along_axis(grid, (jnp.arange(top)[None, :] + turn) % top, axis=1)


def portions_of(number_of, total, most, lean, full):
    weights = [(1 << 20) // math.isqrt(rank ** lean) + 1 for rank in range(1, number_of + 1)]
    largest = most if full else min(most, max(-(-total // number_of), total * weights[0] // sum(weights)))
    least = 1 if total - largest >= number_of - 1 else 0
    counts, rest = [largest] + [least] * (number_of - 1), total - largest - least * (number_of - 1)
    while rest > 0:
        candidates = [i for i in range(1, number_of) if counts[i] < largest] or [i for i in range(1, number_of) if counts[i] < most]
        whole, left = sum([weights[i] for i in candidates]), rest
        for i in candidates:
            addition = min(most - counts[i], max(1, left * weights[i] // whole), rest)
            counts[i] = counts[i] + addition
            rest = rest - addition
    return np.array(counts)


def centred(stream_key, shape, scale, reach, cuts=(), kind=jnp.bfloat16):
    array = scale * jax.random.normal(stream_key, shape, jnp.float32)
    if cuts:
        array = array * shard_levels(stream_key, shape, cuts, -0.22, 0.18)
    return jnp.clip(array, -reach, reach).astype(kind)


def setup_inputs(seed: int = 0) -> dict:
    splits = jax.random.split(jax.random.key(seed), 5)
    queries = draw_queries(jax.random.fold_in(splits[4], 71), 0)
    bank = centred(splits[1], (CLUSTERS, R, D), D ** -0.5, 0.21875, ((0, 32), (1, 4)))
    labels = touch_ends(jax.random.randint(splits[2], (CLUSTERS, R), 0, CLASSES), jax.random.fold_in(splits[2], 1), 0, CLASSES - 1).astype(jnp.int32)
    probes_keys = jax.random.split(jax.random.fold_in(splits[3], 1), QUERIES // Q_DEV)
    probes_turns = jax.random.permutation(jax.random.fold_in(splits[3], 3), QUERIES // Q_DEV)
    probes = jax.vmap(lambda own, number: routed_block(jax.random.fold_in(splits[3], 2), own, number, Q_DEV, CLUSTERS, P_SIZE, CAP, 2))(probes_keys, probes_turns).reshape((QUERIES, P_SIZE))
    return dict(queries=queries, bank=bank, labels=labels, probes=probes)


logit_scale = 2.0


def reference(queries, bank, labels, probes):
    limit = CAP * N_DP * N_REP
    class_iota = jnp.arange(CLASSES, dtype=jnp.int32)

    def visit(carry, cluster):
        top_now, total_now, tally_now = carry
        member = jnp.any(probes == cluster, axis=1)
        order = jnp.argsort(jnp.where(member, 0, 1).astype(jnp.int32), stable=True)[:limit].astype(jnp.int32)
        valid = member[order]
        picked = queries[order]
        cluster_rows = lax.dynamic_index_in_dim(bank, cluster, 0, keepdims=False)
        row_labels = lax.dynamic_index_in_dim(labels, cluster, 0, keepdims=False)
        scores = logit_scale * jnp.dot(picked, cluster_rows.T, preferred_element_type=jnp.float32)
        highest = jnp.max(scores, axis=1)
        weights = jnp.exp(scores - highest[:, None])
        totals = jnp.sum(weights, axis=1)
        weights_half = weights.astype(jnp.bfloat16)
        one_hot = (row_labels[:, None] == class_iota[None, :]).astype(jnp.bfloat16)
        tallies = jnp.dot(weights_half, one_hot, preferred_element_type=jnp.float32)
        old_top = top_now[order]
        new_top = jnp.where(valid, jnp.maximum(old_top, highest), old_top)
        keep_weight = jnp.exp(old_top - new_top)
        add_weight = jnp.where(valid, jnp.exp(highest - new_top), jnp.zeros_like(highest))
        new_total = total_now[order] * keep_weight + totals * add_weight
        new_tally = tally_now[order] * keep_weight[:, None] + tallies * add_weight[:, None]
        return (top_now.at[order].set(new_top), total_now.at[order].set(new_total), tally_now.at[order].set(new_tally)), None

    start_state = (jnp.full((QUERIES,), -1.0e30, jnp.float32), jnp.zeros((QUERIES,), jnp.float32), jnp.zeros((QUERIES, CLASSES), jnp.float32))
    final_state, _ = lax.scan(visit, start_state, jnp.arange(CLUSTERS, dtype=jnp.int32))
    return CLASSES * final_state[2] / final_state[1][:, None]
```

```python
import jax
import jax.numpy as jnp
import numpy as np
from jax import lax
from jax.experimental import pallas as pl
from jax.experimental.pallas import tpu as pltpu
from jax.sharding import PartitionSpec as P

CLASSES = 128
SLOTS = 4
ROWS = 40
NEG = -1.0e30
BOTH = ("dp", "rep")

STRIDE = {"x": 1, "y": 32, "z": 8}
ORDERS = ("xyz", "yzx", "zxy")
BF, F32 = jnp.bfloat16, jnp.float32


def moves(axis, target):
    stride = STRIDE[axis]
    pairs = []
    for d in range(128):
        at = d // stride % 4
        pairs.append((d, d + (target(at) - at) * stride))
    return pairs


def shift(value, axis, step):
    return lax.ppermute(value, BOTH, moves(axis, lambda at: (at + step) % 4))


def swap(value, axis, mask):
    return lax.ppermute(value, BOTH, moves(axis, lambda at: at ^ mask))


def dot_t(a, b):
    return lax.dot_general(a, b, (((1,), (1,)), ((), ())), preferred_element_type=F32)


def iota(shape, dim):
    return lax.broadcasted_iota(jnp.int32, shape, dim)


def route_kernel(q_ref, probes_ref, c0_ref, c1_ref, c2_ref, code_ref):
    probes = probes_ref[...].astype(F32)
    eye = (iota((64, 64), 0) == iota((64, 64), 1)).astype(BF)
    cols = dot_t(eye, probes.astype(BF))
    earlier = iota((64, 64), 0) < iota((64, 64), 1)
    ranks = []
    for p in range(8):
        same = jnp.zeros((64, 64), F32)
        for o in range(8):
            same += (cols[:, o : o + 1] == probes[p : p + 1, :]).astype(F32)
        ranks.append(jnp.sum(jnp.where(earlier, same, 0.0), axis=0, keepdims=True))
    rank = jnp.concatenate(ranks, axis=0)
    code_ref[...] = 4.0 * cols + dot_t(eye, rank.astype(BF))
    spread = (iota((64, 256), 0) == iota((64, 256), 1) % 64).astype(BF)
    c0_ref[0:64, :] = q_ref[:, 0:256]
    c1_ref[0:64, :] = q_ref[:, 256:512]
    c2_ref[0:64, :] = q_ref[:, 512:768]
    c0_ref[64:72, :] = jnp.dot(probes.astype(BF), spread, preferred_element_type=F32).astype(BF)
    c1_ref[64:72, :] = jnp.dot(rank.astype(BF), spread, preferred_element_type=F32).astype(BF)
    c2_ref[64:72, :] = jnp.zeros((8, 256), BF)


def route(queries, probes_t):
    chunk = jax.ShapeDtypeStruct((72, 256), BF)
    return pl.pallas_call(
        route_kernel,
        out_shape=(chunk, chunk, chunk, jax.ShapeDtypeStruct((64, 8), F32)),
        name="route",
    )(queries, probes_t)


def gather(chunks):
    held = [c[None] for c in chunks]
    for stage in range(2):
        axes = [ORDERS[k][stage] for k in range(3)]
        one = [swap(held[k], axes[k], 1) for k in range(3)]
        held = [jnp.concatenate([held[k], one[k]]) for k in range(3)]
        two = [swap(held[k], axes[k], 3) for k in range(3)]
        held = [jnp.concatenate([held[k], two[k]]) for k in range(3)]
    axes = [ORDERS[k][2] for k in range(3)]
    up = [shift(held[k], axes[k], -1) for k in range(3)]
    down = [shift(held[k], axes[k], 1) for k in range(3)]
    far_a = [shift(up[k][:, :, :128], axes[k], -1) for k in range(3)]
    far_b = [shift(down[k][:, :, 128:], axes[k], 1) for k in range(3)]
    return [(held[k], up[k], far_a[k], far_b[k], down[k]) for k in range(3)]


def pick_kernel(where, *refs):
    pieces = [refs[5 * k : 5 * k + 5] for k in range(3)]
    own_ref, other_ref = refs[15], refs[16]
    lane = iota((16, 256), 1) // 64
    row = iota((16, 256), 0)
    source = jnp.where(
        lane == 0, where[0], jnp.where(lane == 1, where[1], jnp.where(lane == 2, where[2], where[3]))
    )
    want = jnp.where(row // 4 == source, row % 4 + 1, -1).astype(F32)
    part = iota((8, 256), 1) // 64
    cluster = iota((8, 256), 0)
    bases = [(where[24] * 8 + cluster).astype(F32), (where[25] * 8 + cluster).astype(F32)]

    def block(k, rx, ry, rz, aux):
        r = (rx, ry, rz)
        order = ["xyz".index(a) for a in ORDERS[k]]
        at = where[12 + 4 * order[1] + r[order[1]]] * 4 + where[12 + 4 * order[0] + r[order[0]]]
        far = r[order[2]]
        rows = slice(64, 72) if aux else slice(0, 64)
        if far == 2:
            return jnp.concatenate([pieces[k][2][at, rows, :], pieces[k][3][at, rows, :]], axis=1)
        return pieces[k][{0: 0, 1: 1, 3: 4}[far]][at, rows, :]

    def aux_of(k, ry, rz):
        a = [block(k, rx, ry, rz, True).astype(F32) for rx in range(4)]
        return jnp.where(part == 0, a[0], jnp.where(part == 1, a[1], jnp.where(part == 2, a[2], a[3])))

    for ry in range(4):
        for rz in range(4):
            probe = aux_of(0, ry, rz)
            rank = aux_of(1, ry, rz)
            picks = []
            for g in range(2):
                slot = jnp.zeros((8, 256), F32)
                for p in range(8):
                    slot += jnp.where(probe[p : p + 1, :] == bases[g], rank[p : p + 1, :] + 1.0, 0.0)
                for c in range(8):
                    picks.append(jnp.where(slot[c : c + 1, :] == want, 2.0, 0.0).astype(BF))
            pick = jnp.concatenate(picks, axis=0)
            base = pl.multiple_of((where[4 + ry] * 4 + where[8 + rz]) * 16, 16)
            for k in range(3):
                rows = jnp.concatenate([block(k, rx, ry, rz, False) for rx in range(4)], axis=0)
                found = jnp.dot(pick, rows, preferred_element_type=F32).astype(BF)
                for c in range(8):
                    own_ref[c, pl.ds(base, 16), 256 * k : 256 * k + 256] = found[16 * c : 16 * c + 16]
                    other_ref[c, pl.ds(base, 16), 256 * k : 256 * k + 256] = found[
                        128 + 16 * c : 144 + 16 * c
                    ]


def pick(where, pieces):
    flat = [a for p in pieces for a in p]
    out = jax.ShapeDtypeStruct((8, 256, 768), BF)
    vmem = pl.BlockSpec(memory_space=pltpu.VMEM)
    return pl.pallas_call(
        pick_kernel,
        out_shape=(out, out),
        in_specs=[pl.BlockSpec(memory_space=pltpu.SMEM)] + [vmem] * 15,
        out_specs=(vmem, vmem),
        name="pick",
    )(where, *flat)


def score_body(where, p_ref, bank_ref, labels_ref, acc, tal, shifts, wide):
    c = pl.program_id(0)
    s = dot_t(p_ref[0], bank_ref[0])
    top = jnp.max(s, axis=1, keepdims=True)
    high = top.astype(BF).astype(F32)
    m = high + (top - high).astype(BF).astype(F32)
    e = jnp.exp(s - m).astype(BF)
    onehot = (labels_ref[pl.ds(c, 1), :] == iota((CLASSES, 1024), 0)).astype(F32).astype(BF)
    tal[...] = dot_t(e, onehot)
    wide[...] = jnp.broadcast_to(m, (256, 128))

    @pl.when(c == 0)
    def _():
        shifts[...] = jnp.zeros_like(shifts)
        for j in range(34, ROWS):
            acc[pl.ds(j, 64, stride=ROWS), :] = jnp.zeros((64, 128), F32)

    lane = iota((64, 128), 1)
    for j in range(SLOTS):
        acc[pl.ds(c * SLOTS + j, 64, stride=ROWS), :] = tal[pl.ds(j, 64, stride=SLOTS), :]
        shifts[...] = jnp.where(
            lane == where[26] * 32 + c * SLOTS + j, wide[pl.ds(j, 64, stride=SLOTS), :], shifts[...]
        )

    @pl.when(c == pl.num_programs(0) - 1)
    def _():
        full = shifts[...]
        first = full.astype(BF).astype(F32)
        acc[pl.ds(32, 64, stride=ROWS), :] = first
        acc[pl.ds(33, 64, stride=ROWS), :] = full - first


def score_own_kernel(where, p_ref, bank_ref, labels_ref, out_ref, acc, tal, shifts, wide):
    score_body(where, p_ref, bank_ref, labels_ref, acc, tal, shifts, wide)

    @pl.when(pl.program_id(0) == pl.num_programs(0) - 1)
    def _():
        out_ref[...] = acc[...].astype(BF)


def score_other_kernel(where, p_ref, bank_ref, labels_ref, own_ref, out_ref, acc, tal, shifts, wide):
    score_body(where, p_ref, bank_ref, labels_ref, acc, tal, shifts, wide)

    @pl.when(pl.program_id(0) == pl.num_programs(0) - 1)
    def _():
        size = 4 * ROWS
        for yz in range(16):
            mine = pl.multiple_of((yz * 2 + where[27]) * size, 16)
            theirs = pl.multiple_of((yz * 2 + 1 - where[27]) * size, 16)
            out_ref[pl.ds(mine, size), :] = own_ref[yz * size : yz * size + size, :]
            out_ref[pl.ds(theirs, size), :] = acc[yz * size : yz * size + size, :].astype(BF)


def score(where, picked, bank, labels, own=None):
    clusters, rows, width = bank.shape
    count = picked.shape[1]
    specs = [
        pl.BlockSpec(memory_space=pltpu.SMEM),
        pl.BlockSpec((1, count, width), lambda c: (c, 0, 0)),
        pl.BlockSpec((1, rows, width), lambda c: (c, 0, 0)),
        pl.BlockSpec((clusters, rows), lambda c: (0, 0)),
    ]
    args = [where, picked, bank, labels]
    out_rows = 64 * ROWS
    if own is not None:
        specs.append(pl.BlockSpec((64 * ROWS, 128), lambda c: (0, 0)))
        args.append(own)
        out_rows = 128 * ROWS
    return pl.pallas_call(
        score_own_kernel if own is None else score_other_kernel,
        grid=(clusters,),
        out_shape=jax.ShapeDtypeStruct((out_rows, 128), BF),
        in_specs=specs,
        out_specs=pl.BlockSpec((out_rows, 128), lambda c: (0, 0)),
        scratch_shapes=[
            pltpu.VMEM((64 * ROWS, 128), F32),
            pltpu.VMEM((256, 128), F32),
            pltpu.VMEM((64, 128), F32),
            pltpu.VMEM((256, 128), F32),
        ],
        cost_estimate=pl.CostEstimate(
            flops=2 * clusters * count * rows * (width + 128),
            transcendentals=clusters * count * rows,
            bytes_accessed=bank.size * 2,
        ),
        name="score_own" if own is None else "score_other",
    )(*args)


def fold_kernel(code_ref, parts_ref, out_ref, marked):
    slot = (iota((64, 128), 1) % 32).astype(F32)
    codes = [jnp.broadcast_to(code_ref[:, p : p + 1], (64, 128)) for p in range(8)]
    best = jnp.full((64, 128), NEG, F32)
    for g in range(32):
        rows = parts_ref[4 * g, 32:40, :].astype(F32)
        for r in range(1, 4):
            rows += parts_ref[4 * g + r, 32:40, :].astype(F32)
        m = rows[0:1, :] + rows[1:2, :]
        here = slot + 32.0 * g
        hit = codes[0] == here
        for p in range(1, 8):
            hit = jnp.logical_or(hit, codes[p] == here)
        value = jnp.where(hit, m, NEG)
        marked[g] = value
        best = jnp.maximum(best, value)
    top = jnp.max(best, axis=1, keepdims=True)
    total = jnp.zeros((128, 128), F32)
    for g in range(0, 32, 2):
        pair = []
        for h in range(2):
            w = jnp.exp(marked[g + h] - top)
            first = w.astype(BF)
            pair.append(jnp.concatenate([first, (w - first.astype(F32)).astype(BF)], axis=0))
        weights = jnp.concatenate(pair, axis=1)
        tallies = jnp.concatenate([parts_ref[4 * g + r, 0:32, :] for r in range(8)], axis=0)
        total += jnp.dot(weights, tallies, preferred_element_type=F32)
    votes = total[0:64] + total[64:128]
    out_ref[...] = CLASSES * votes / jnp.sum(votes, axis=1, keepdims=True)


def fold(codes, parts):
    return pl.pallas_call(
        fold_kernel,
        out_shape=jax.ShapeDtypeStruct((64, CLASSES), F32),
        scratch_shapes=[pltpu.VMEM((32, 64, 128), F32)],
        name="fold",
    )(codes, parts)


def table():
    dp, x = lax.axis_index("dp"), lax.axis_index("rep")
    y, z, core = dp // 8, dp // 2 % 4, dp % 2
    ring = jnp.arange(4, dtype=jnp.int32)
    place = []
    coords = []
    for me in (x, y, z):
        at = (me + ring) % 4
        apart = at ^ me
        coords.append(at)
        place.append(apart ^ (apart >> 1))
    tail = jnp.stack([dp, dp ^ 1, x, core]).astype(jnp.int32)
    return jnp.concatenate(coords + place + [tail]).astype(jnp.int32)


def local(queries, bank, labels, probes):
    where = table()
    c0, c1, c2, codes = route(queries, probes.T)
    own, other = pick(where, gather((c0, c1, c2)))
    arrived = lax.ppermute(other, BOTH, [(d, d ^ 4) for d in range(128)])
    mine = score(where, own, bank, labels)
    blocks = score(where, arrived, bank, labels, mine)
    parts = lax.all_to_all(
        blocks.reshape(128, ROWS, 128), BOTH, split_axis=0, concat_axis=0, tiled=True
    )
    return fold(codes, parts)


def solution(mesh):
    return jax.shard_map(
        local,
        mesh=mesh,
        in_specs=(
            P(BOTH, None),
            P("dp", "rep", None),
            P("dp", "rep"),
            P(BOTH, None),
        ),
        out_specs=P(BOTH, None),
        check_vma=False,
    )
```

```python
import functools

import jax
import jax.numpy as jnp
from jax import lax
from jax.experimental import pallas as pl
from jax.experimental.pallas import tpu as pltpu
from jax.sharding import PartitionSpec as P

CLASSES = 128
SLOTS = 4
ROWS = 40
NEG = -1.0e30
BOTH = ("dp", "rep")
UNROLL = 1

STRIDE = {"x": 1, "y": 32, "z": 8}
ORDERS = ("xyz", "yzx", "zxy")
BF, F32 = jnp.bfloat16, jnp.float32


def moves(axis, target):
    stride = STRIDE[axis]
    pairs = []
    for d in range(128):
        at = d // stride % 4
        pairs.append((d, d + (target(at) - at) * stride))
    return pairs


def shift(value, axis, step):
    return lax.ppermute(value, BOTH, moves(axis, lambda at: (at + step) % 4))


def swap(value, axis, mask):
    return lax.ppermute(value, BOTH, moves(axis, lambda at: at ^ mask))


def dot_t(a, b):
    return lax.dot_general(a, b, (((1,), (1,)), ((), ())), preferred_element_type=F32)


def near(value):
    return pltpu.with_memory_space_constraint(value, pltpu.VMEM)


def grant(mib):
    return pltpu.CompilerParams(vmem_limit_bytes=mib << 20)


VMEM = pl.BlockSpec(memory_space=pltpu.VMEM)


def iota(shape, dim):
    return lax.broadcasted_iota(jnp.int32, shape, dim)


def route_kernel(q_ref, probes_ref, c0_ref, c1_ref, c2_ref, code_ref):
    probes = probes_ref[...].astype(F32)
    eye = (iota((64, 64), 0) == iota((64, 64), 1)).astype(BF)
    cols = dot_t(eye, probes.astype(BF))
    earlier = iota((64, 64), 0) < iota((64, 64), 1)
    ranks = []
    for p in range(8):
        same = jnp.zeros((64, 64), F32)
        for o in range(8):
            same += (cols[:, o : o + 1] == probes[p : p + 1, :]).astype(F32)
        ranks.append(jnp.sum(jnp.where(earlier, same, 0.0), axis=0, keepdims=True))
    rank = jnp.concatenate(ranks, axis=0)
    code_ref[...] = 4.0 * cols + dot_t(eye, rank.astype(BF))
    spread = (iota((64, 256), 0) == iota((64, 256), 1) % 64).astype(BF)
    c0_ref[0:64, :] = q_ref[:, 0:256]
    c1_ref[0:64, :] = q_ref[:, 256:512]
    c2_ref[0:64, :] = q_ref[:, 512:768]
    c0_ref[64:72, :] = jnp.dot(probes.astype(BF), spread, preferred_element_type=F32).astype(BF)
    c1_ref[64:72, :] = jnp.dot(rank.astype(BF), spread, preferred_element_type=F32).astype(BF)
    c2_ref[64:72, :] = jnp.zeros((8, 256), BF)


def route(queries, probes_t):
    return pl.pallas_call(
        route_kernel,
        out_shape=[pltpu.VMEM((72, 256), BF)] * 3 + [pltpu.VMEM((64, 8), F32)],
        in_specs=[VMEM] * 2,
        out_specs=[VMEM] * 4,
        compiler_params=grant(4),
        name="route",
    )(queries, probes_t)


def join_kernel(a_ref, b_ref, out_ref):
    size = a_ref.shape[0]
    out_ref[0:size] = a_ref[...]
    out_ref[size : 2 * size] = b_ref[...]


def join(a, b):
    return pl.pallas_call(
        join_kernel,
        out_shape=pltpu.VMEM((2 * a.shape[0],) + a.shape[1:], a.dtype),
        in_specs=[VMEM] * 2,
        out_specs=VMEM,
        compiler_params=grant(4),
        name="join",
    )(near(a), near(b))


def half_kernel(at, a_ref, out_ref):
    out_ref[...] = a_ref[at : at + out_ref.shape[0]]


def half(a, at):
    return pl.pallas_call(
        functools.partial(half_kernel, at),
        out_shape=pltpu.VMEM((a.shape[0] // 2,) + a.shape[1:], a.dtype),
        in_specs=[VMEM],
        out_specs=VMEM,
        compiler_params=grant(4),
        name="half",
    )(near(a))


def gather(chunks):
    held = [c[None] for c in chunks]
    for stage in range(2):
        axes = [ORDERS[k][stage] for k in range(3)]
        for mask in (1, 3):
            other = [swap(held[k], axes[k], mask) for k in range(3)]
            held = [join(held[k], other[k]) for k in range(3)]
    axes = [ORDERS[k][2] for k in range(3)]
    up = [shift(held[k], axes[k], -1) for k in range(3)]
    down = [shift(held[k], axes[k], 1) for k in range(3)]
    far_a = [shift(half(up[k], 0), axes[k], -1) for k in range(3)]
    far_b = [shift(half(down[k], 8), axes[k], 1) for k in range(3)]
    return [(held[k], up[k], far_a[k], far_b[k], down[k]) for k in range(3)]


def position():
    dp, x = lax.axis_index("dp"), lax.axis_index("rep")
    return dp, (x, dp // 8, dp // 2 % 4), dp % 2


def pick_kernel(*refs):
    dp, here, _ = position()
    coords = [[(me + r) % 4 for r in range(4)] for me in here]
    apart = [[at ^ me for at in ats] for ats, me in zip(coords, here)]
    place = [[d ^ (d >> 1) for d in ds] for ds in apart]
    pieces = [refs[5 * k : 5 * k + 5] for k in range(3)]
    bank_hbm, own_ref, other_ref, bank_ref, far, sems = refs[15:]
    loads = [pltpu.make_async_copy(bank_hbm.at[c], bank_ref.at[c], sems.at[c]) for c in range(8)]
    for load in loads:
        load.start()
    for k in range(3):
        far[k, 0:8] = pieces[k][2][...]
        far[k, 8:16] = pieces[k][3][...]
    lane = iota((16, 256), 1) // 64
    row = iota((16, 256), 0)
    source = jnp.where(
        lane == 0,
        coords[0][0],
        jnp.where(lane == 1, coords[0][1], jnp.where(lane == 2, coords[0][2], coords[0][3])),
    )
    want = jnp.where(row // 4 == source, row % 4 + 1, -1).astype(F32)
    part = iota((8, 256), 1) // 64
    cluster = iota((8, 256), 0)
    bases = [(dp * 8 + cluster).astype(F32), ((dp ^ 1) * 8 + cluster).astype(F32)]

    def block(k, rx, ry, rz, aux):
        r = (rx, ry, rz)
        order = ["xyz".index(a) for a in ORDERS[k]]
        at = place[order[1]][r[order[1]]] * 4 + place[order[0]][r[order[0]]]
        last = r[order[2]]
        rows = slice(64, 72) if aux else slice(0, 64)
        if last == 2:
            return far[k, at, rows, :]
        return pieces[k][{0: 0, 1: 1, 3: 4}[last]][at, rows, :]

    def aux_of(k, ry, rz):
        a = [block(k, rx, ry, rz, True).astype(F32) for rx in range(4)]
        return jnp.where(part == 0, a[0], jnp.where(part == 1, a[1], jnp.where(part == 2, a[2], a[3])))

    for ry in range(4):
        for rz in range(4):
            probe = aux_of(0, ry, rz)
            rank = aux_of(1, ry, rz)
            picks = []
            for g in range(2):
                slot = jnp.zeros((8, 256), F32)
                for p in range(8):
                    slot += jnp.where(probe[p : p + 1, :] == bases[g], rank[p : p + 1, :] + 1.0, 0.0)
                for c in range(8):
                    picks.append(jnp.where(slot[c : c + 1, :] == want, 2.0, 0.0).astype(BF))
            pick = jnp.concatenate(picks, axis=0)
            base = pl.multiple_of((coords[1][ry] * 4 + coords[2][rz]) * 16, 16)
            for k in range(3):
                rows = jnp.concatenate([block(k, rx, ry, rz, False) for rx in range(4)], axis=0)
                found = jnp.dot(pick, rows, preferred_element_type=F32).astype(BF)
                for c in range(8):
                    own_ref[c, pl.ds(base, 16), 256 * k : 256 * k + 256] = found[16 * c : 16 * c + 16]
                    other_ref[c, pl.ds(base, 16), 256 * k : 256 * k + 256] = found[
                        128 + 16 * c : 144 + 16 * c
                    ]
    for load in loads:
        load.wait()


def pick(pieces, bank):
    flat = [near(a) for p in pieces for a in p]
    out = pltpu.VMEM((8, 256, 768), BF)
    return pl.pallas_call(
        pick_kernel,
        out_shape=(out, out, pltpu.VMEM(bank.shape, BF)),
        in_specs=[VMEM] * 15 + [pl.BlockSpec(memory_space=pltpu.HBM)],
        out_specs=(VMEM, VMEM, VMEM),
        scratch_shapes=[pltpu.VMEM((3, 16, 72, 256), BF), pltpu.SemaphoreType.DMA((8,))],
        compiler_params=grant(12),
        name="pick",
    )(*flat, pltpu.with_memory_space_constraint(bank, pltpu.HBM))


def score_body(p_ref, bank_ref, labels_ref, acc, tal, wide, shifts):
    clusters = p_ref.shape[0]
    lane = iota((64, 128), 1) - lax.axis_index("rep") * 32
    shifts[...] = jnp.zeros_like(shifts)

    def one(c, carry):
        s = dot_t(bank_ref[c], p_ref[c])
        top = jnp.max(s, axis=0, keepdims=True)
        high = top.astype(BF).astype(F32)
        m = high + (top - high).astype(BF).astype(F32)
        e = jnp.exp(s - m).astype(BF)
        onehot = (labels_ref[pl.ds(c, 1), :] == iota((CLASSES, 1024), 0)).astype(F32).astype(BF)
        tal[...] = jnp.dot(onehot, e, preferred_element_type=F32).T
        wide[...] = jnp.broadcast_to(m, (128, 256)).T
        for j in range(SLOTS):
            acc[pl.ds(c * SLOTS + j, 64, stride=ROWS), :] = tal[pl.ds(j, 64, stride=SLOTS), :]
            shifts[...] = jnp.where(
                lane == c * SLOTS + j, wide[pl.ds(j, 64, stride=SLOTS), :], shifts[...]
            )
        return carry

    lax.fori_loop(0, clusters, one, 0, unroll=UNROLL)
    full = shifts[...]
    first = full.astype(BF).astype(F32)
    acc[pl.ds(32, 64, stride=ROWS), :] = first
    acc[pl.ds(33, 64, stride=ROWS), :] = full - first
    for j in range(34, ROWS):
        acc[pl.ds(j, 64, stride=ROWS), :] = jnp.zeros((64, 128), F32)


def score_own_kernel(p_ref, bank_ref, labels_ref, out_ref, *scratch):
    score_body(p_ref, bank_ref, labels_ref, *scratch)
    out_ref[...] = scratch[0][...].astype(BF)


def score_other_kernel(p_ref, bank_ref, labels_ref, own_ref, out_ref, *scratch):
    score_body(p_ref, bank_ref, labels_ref, *scratch)
    acc, core = scratch[0], position()[2]
    size = 4 * ROWS
    for yz in range(16):
        mine = pl.multiple_of((yz * 2 + core) * size, 16)
        theirs = pl.multiple_of((yz * 2 + 1 - core) * size, 16)
        out_ref[pl.ds(mine, size), :] = own_ref[yz * size : yz * size + size, :]
        out_ref[pl.ds(theirs, size), :] = acc[yz * size : yz * size + size, :].astype(BF)


def score(picked, bank, labels, own=None):
    clusters, rows, width = bank.shape
    count = picked.shape[1]
    args = [near(picked), near(bank), near(labels)]
    out_rows = 64 * ROWS
    if own is not None:
        args.append(near(own))
        out_rows = 128 * ROWS
    return pl.pallas_call(
        score_own_kernel if own is None else score_other_kernel,
        out_shape=pltpu.VMEM((out_rows, 128), BF),
        in_specs=[VMEM] * len(args),
        out_specs=VMEM,
        scratch_shapes=[
            pltpu.VMEM((64 * ROWS, 128), F32),
            pltpu.VMEM((256, 128), F32),
            pltpu.VMEM((256, 128), F32),
            pltpu.VMEM((64, 128), F32),
        ],
        compiler_params=grant(12),
        cost_estimate=pl.CostEstimate(
            flops=2 * clusters * count * rows * (width + 128),
            transcendentals=clusters * count * rows,
            bytes_accessed=bank.size * 2,
        ),
        name="score_own" if own is None else "score_other",
    )(*args)


def fold_kernel(code_ref, parts_ref, out_ref, marked):
    slot = (iota((64, 128), 1) % 32).astype(F32)
    codes = [jnp.broadcast_to(code_ref[:, p : p + 1], (64, 128)) for p in range(8)]
    best = jnp.full((64, 128), NEG, F32)
    for g in range(32):
        rows = parts_ref[4 * g, 32:40, :].astype(F32)
        for r in range(1, 4):
            rows += parts_ref[4 * g + r, 32:40, :].astype(F32)
        m = rows[0:1, :] + rows[1:2, :]
        here = slot + 32.0 * g
        hit = codes[0] == here
        for p in range(1, 8):
            hit = jnp.logical_or(hit, codes[p] == here)
        value = jnp.where(hit, m, NEG)
        marked[g] = value
        best = jnp.maximum(best, value)
    top = jnp.max(best, axis=1, keepdims=True)
    total = jnp.zeros((128, 128), F32)
    for g in range(0, 32, 2):
        pair = []
        for h in range(2):
            w = jnp.exp(marked[g + h] - top)
            first = w.astype(BF)
            pair.append(jnp.concatenate([first, (w - first.astype(F32)).astype(BF)], axis=0))
        weights = jnp.concatenate(pair, axis=1)
        tallies = jnp.concatenate([parts_ref[4 * g + r, 0:32, :] for r in range(8)], axis=0)
        total += jnp.dot(weights, tallies, preferred_element_type=F32)
    votes = total[0:64] + total[64:128]
    out_ref[...] = CLASSES * votes / jnp.sum(votes, axis=1, keepdims=True)


def fold(codes, parts):
    return pl.pallas_call(
        fold_kernel,
        out_shape=jax.ShapeDtypeStruct((64, CLASSES), F32),
        in_specs=[VMEM] * 2,
        out_specs=VMEM,
        scratch_shapes=[pltpu.VMEM((32, 64, 128), F32)],
        compiler_params=grant(8),
        name="fold",
    )(near(codes), near(parts))


def local(queries, bank, labels, probes):
    *chunks, codes = route(queries, probes.T)
    own, other, bank = pick(gather(chunks), bank)
    arrived = lax.ppermute(other, BOTH, [(d, d ^ 4) for d in range(128)])
    mine = score(own, bank, labels)
    blocks = score(arrived, bank, labels, mine)
    parts = lax.all_to_all(
        blocks.reshape(128, ROWS, 128), BOTH, split_axis=0, concat_axis=0, tiled=True
    )
    return fold(codes, parts)


def solution(mesh):
    return jax.shard_map(
        local,
        mesh=mesh,
        in_specs=(
            P(BOTH, None),
            P("dp", "rep", None),
            P("dp", "rep"),
            P(BOTH, None),
        ),
        out_specs=P(BOTH, None),
        check_vma=False,
    )
```

```python
import functools

import jax
import jax.numpy as jnp
from jax import lax
from jax.experimental import pallas as pl
from jax.experimental.pallas import tpu as pltpu
from jax.sharding import PartitionSpec as P

CLASSES = 128
SLOTS = 4
ROWS = 40
NEG = -1.0e30
BOTH = ("dp", "rep")

STRIDE = {"x": 1, "y": 32, "z": 8}
ORDERS = ("xyz", "yzx", "zxy")
BF, F32 = jnp.bfloat16, jnp.float32


def moves(axis, target):
    stride = STRIDE[axis]
    pairs = []
    for d in range(128):
        at = d // stride % 4
        pairs.append((d, d + (target(at) - at) * stride))
    return pairs


def shift(value, axis, step):
    return lax.ppermute(value, BOTH, moves(axis, lambda at: (at + step) % 4))


def swap(value, axis, mask):
    return lax.ppermute(value, BOTH, moves(axis, lambda at: at ^ mask))


def dot_t(a, b):
    return lax.dot_general(a, b, (((1,), (1,)), ((), ())), preferred_element_type=F32)


def near(value):
    return pltpu.with_memory_space_constraint(value, pltpu.VMEM)


def grant(mib):
    return pltpu.CompilerParams(vmem_limit_bytes=mib << 20)


VMEM = pl.BlockSpec(memory_space=pltpu.VMEM)


def iota(shape, dim):
    return lax.broadcasted_iota(jnp.int32, shape, dim)


def route_kernel(q_ref, probes_ref, c0_ref, c1_ref, c2_ref, code_ref, sems):
    loads = []
    for k, c_ref in enumerate((c0_ref, c1_ref, c2_ref)):
        columns = q_ref.at[:, 256 * k : 256 * k + 256]
        loads.append(pltpu.make_async_copy(columns, c_ref.at[0:64, :], sems.at[k]))
        loads[k].start()
    probes = probes_ref[...].astype(F32)
    eye = (iota((64, 64), 0) == iota((64, 64), 1)).astype(BF)
    cols = dot_t(eye, probes.astype(BF))
    earlier = iota((64, 64), 0) < iota((64, 64), 1)
    ranks = []
    for p in range(8):
        same = jnp.zeros((64, 64), F32)
        for o in range(8):
            same += (cols[:, o : o + 1] == probes[p : p + 1, :]).astype(F32)
        ranks.append(jnp.sum(jnp.where(earlier, same, 0.0), axis=0, keepdims=True))
    rank = jnp.concatenate(ranks, axis=0)
    code_ref[...] = 4.0 * cols + dot_t(eye, rank.astype(BF))
    spread = (iota((64, 256), 0) == iota((64, 256), 1) % 64).astype(BF)
    c0_ref[64:72, :] = jnp.dot(probes.astype(BF), spread, preferred_element_type=F32).astype(BF)
    c1_ref[64:72, :] = jnp.dot(rank.astype(BF), spread, preferred_element_type=F32).astype(BF)
    c2_ref[64:72, :] = jnp.zeros((8, 256), BF)
    for load in loads:
        load.wait()


def route(queries, probes_t):
    return pl.pallas_call(
        route_kernel,
        out_shape=[pltpu.VMEM((72, 256), BF)] * 3 + [pltpu.VMEM((64, 8), F32)],
        in_specs=[pl.BlockSpec(memory_space=pltpu.HBM), VMEM],
        out_specs=[VMEM] * 4,
        scratch_shapes=[pltpu.SemaphoreType.DMA((3,))],
        compiler_params=grant(4),
        name="route",
    )(pltpu.with_memory_space_constraint(queries, pltpu.HBM), probes_t)


def join_kernel(a_ref, b_ref, out_ref):
    size = a_ref.shape[0]
    out_ref[0:size] = a_ref[...]
    out_ref[size : 2 * size] = b_ref[...]


def join(a, b):
    return pl.pallas_call(
        join_kernel,
        out_shape=pltpu.VMEM((2 * a.shape[0],) + a.shape[1:], a.dtype),
        in_specs=[VMEM] * 2,
        out_specs=VMEM,
        compiler_params=grant(4),
        name="join",
    )(near(a), near(b))


def half_kernel(at, a_ref, out_ref):
    out_ref[...] = a_ref[at : at + out_ref.shape[0]]


def half(a, at):
    return pl.pallas_call(
        functools.partial(half_kernel, at),
        out_shape=pltpu.VMEM((a.shape[0] // 2,) + a.shape[1:], a.dtype),
        in_specs=[VMEM],
        out_specs=VMEM,
        compiler_params=grant(4),
        name="half",
    )(near(a))


def gather(chunks):
    held = [c[None] for c in chunks]
    for stage in range(2):
        axes = [ORDERS[k][stage] for k in range(3)]
        for mask in (1, 3):
            other = [swap(held[k], axes[k], mask) for k in range(3)]
            held = [join(held[k], other[k]) for k in range(3)]
    axes = [ORDERS[k][2] for k in range(3)]
    up = [shift(held[k], axes[k], -1) for k in range(3)]
    down = [shift(held[k], axes[k], 1) for k in range(3)]
    far_a = [shift(half(up[k], 0), axes[k], -1) for k in range(3)]
    far_b = [shift(half(down[k], 8), axes[k], 1) for k in range(3)]
    return [(held[k], up[k], far_a[k], far_b[k], down[k]) for k in range(3)]


def position():
    dp, x = lax.axis_index("dp"), lax.axis_index("rep")
    return dp, (x, dp // 8, dp // 2 % 4), dp % 2


def pick_kernel(*refs):
    dp, here, _ = position()
    coords = [[(me + r) % 4 for r in range(4)] for me in here]
    apart = [[at ^ me for at in ats] for ats, me in zip(coords, here)]
    place = [[d ^ (d >> 1) for d in ds] for ds in apart]
    pieces = [refs[5 * k : 5 * k + 5] for k in range(3)]
    own_ref, other_ref, far = refs[15:]
    for k in range(3):
        far[k, 0:8] = pieces[k][2][...]
        far[k, 8:16] = pieces[k][3][...]
    lane = iota((16, 256), 1) // 64
    row = iota((16, 256), 0)
    source = jnp.where(
        lane == 0,
        coords[0][0],
        jnp.where(lane == 1, coords[0][1], jnp.where(lane == 2, coords[0][2], coords[0][3])),
    )
    want = jnp.where(row // 4 == source, row % 4 + 1, -1).astype(F32)
    part = iota((8, 256), 1) // 64
    cluster = iota((8, 256), 0)
    bases = [(dp * 8 + cluster).astype(F32), ((dp ^ 1) * 8 + cluster).astype(F32)]

    def block(k, rx, ry, rz, aux):
        r = (rx, ry, rz)
        order = ["xyz".index(a) for a in ORDERS[k]]
        at = place[order[1]][r[order[1]]] * 4 + place[order[0]][r[order[0]]]
        last = r[order[2]]
        rows = slice(64, 72) if aux else slice(0, 64)
        if last == 2:
            return far[k, at, rows, :]
        return pieces[k][{0: 0, 1: 1, 3: 4}[last]][at, rows, :]

    def aux_of(k, ry, rz):
        a = [block(k, rx, ry, rz, True).astype(F32) for rx in range(4)]
        return jnp.where(part == 0, a[0], jnp.where(part == 1, a[1], jnp.where(part == 2, a[2], a[3])))

    for ry in range(4):
        for rz in range(4):
            probe = aux_of(0, ry, rz)
            rank = aux_of(1, ry, rz)
            picks = []
            for g in range(2):
                slot = jnp.zeros((8, 256), F32)
                for p in range(8):
                    slot += jnp.where(probe[p : p + 1, :] == bases[g], rank[p : p + 1, :] + 1.0, 0.0)
                for c in range(8):
                    picks.append(jnp.where(slot[c : c + 1, :] == want, 2.0, 0.0).astype(BF))
            pick = jnp.concatenate(picks, axis=0)
            base = pl.multiple_of((coords[1][ry] * 4 + coords[2][rz]) * 16, 16)
            for k in range(3):
                rows = jnp.concatenate([block(k, rx, ry, rz, False) for rx in range(4)], axis=0)
                found = jnp.dot(pick, rows, preferred_element_type=F32).astype(BF)
                for c in range(8):
                    own_ref[c, pl.ds(base, 16), 256 * k : 256 * k + 256] = found[16 * c : 16 * c + 16]
                    other_ref[c, pl.ds(base, 16), 256 * k : 256 * k + 256] = found[
                        128 + 16 * c : 144 + 16 * c
                    ]

def pick(pieces):
    flat = [near(a) for p in pieces for a in p]
    out = pltpu.VMEM((8, 256, 768), BF)
    return pl.pallas_call(
        pick_kernel,
        out_shape=(out, out),
        in_specs=[VMEM] * 15,
        out_specs=(VMEM, VMEM),
        scratch_shapes=[pltpu.VMEM((3, 16, 72, 256), BF)],
        compiler_params=grant(12),
        name="pick",
    )(*flat)


def score_body(p_ref, bank_ref, labels_ref, acc, tal, wide, shifts, even, odd):
    clusters = p_ref.shape[0]
    lane = iota((64, 128), 1) - lax.axis_index("rep") * 32
    shifts[...] = jnp.zeros_like(shifts)

    def begin(c, held):
        s = dot_t(bank_ref[c], p_ref[c])
        held[...] = s
        return jnp.max(s, axis=0, keepdims=True)

    def finish(c, held, top):
        high = top.astype(BF).astype(F32)
        m = high + (top - high).astype(BF).astype(F32)
        e = jnp.exp(held[...] - m).astype(BF)
        onehot = (labels_ref[pl.ds(c, 1), :] == iota((CLASSES, 1024), 0)).astype(F32).astype(BF)
        tal[...] = jnp.dot(onehot, e, preferred_element_type=F32).T
        wide[...] = jnp.broadcast_to(m, (128, 256)).T
        for j in range(SLOTS):
            acc[pl.ds(c * SLOTS + j, 64, stride=ROWS), :] = tal[pl.ds(j, 64, stride=SLOTS), :]
            shifts[...] = jnp.where(
                lane == c * SLOTS + j, wide[pl.ds(j, 64, stride=SLOTS), :], shifts[...]
            )

    def two(n, top):
        c = 2 * n
        other = begin(c + 1, odd)
        finish(c, even, top)
        top = begin(c + 2, even)
        finish(c + 1, odd, other)
        return top

    top = lax.fori_loop(0, clusters // 2 - 1, two, begin(0, even))
    other = begin(clusters - 1, odd)
    finish(clusters - 2, even, top)
    finish(clusters - 1, odd, other)
    full = shifts[...]
    first = full.astype(BF).astype(F32)
    acc[pl.ds(32, 64, stride=ROWS), :] = first
    acc[pl.ds(33, 64, stride=ROWS), :] = full - first
    for j in range(34, ROWS):
        acc[pl.ds(j, 64, stride=ROWS), :] = jnp.zeros((64, 128), F32)


def score_own_kernel(p_ref, bank_ref, labels_ref, out_ref, *scratch):
    score_body(p_ref, bank_ref, labels_ref, *scratch)
    out_ref[...] = scratch[0][...].astype(BF)


def score_other_kernel(p_ref, bank_ref, labels_ref, own_ref, out_ref, *scratch):
    score_body(p_ref, bank_ref, labels_ref, *scratch)
    acc, core = scratch[0], position()[2]
    size = 4 * ROWS
    for yz in range(16):
        mine = pl.multiple_of((yz * 2 + core) * size, 16)
        theirs = pl.multiple_of((yz * 2 + 1 - core) * size, 16)
        out_ref[pl.ds(mine, size), :] = own_ref[yz * size : yz * size + size, :]
        out_ref[pl.ds(theirs, size), :] = acc[yz * size : yz * size + size, :].astype(BF)


def score(picked, bank, labels, own=None):
    clusters, rows, width = bank.shape
    count = picked.shape[1]
    args = [near(picked), near(bank), near(labels)]
    out_rows = 64 * ROWS
    if own is not None:
        args.append(near(own))
        out_rows = 128 * ROWS
    return pl.pallas_call(
        score_own_kernel if own is None else score_other_kernel,
        out_shape=pltpu.VMEM((out_rows, 128), BF),
        in_specs=[VMEM] * len(args),
        out_specs=VMEM,
        scratch_shapes=[
            pltpu.VMEM((64 * ROWS, 128), F32),
            pltpu.VMEM((256, 128), F32),
            pltpu.VMEM((256, 128), F32),
            pltpu.VMEM((64, 128), F32),
            pltpu.VMEM((1024, 256), F32),
            pltpu.VMEM((1024, 256), F32),
        ],
        compiler_params=grant(12),
        cost_estimate=pl.CostEstimate(
            flops=2 * clusters * count * rows * (width + 128),
            transcendentals=clusters * count * rows,
            bytes_accessed=bank.size * 2,
        ),
        name="score_own" if own is None else "score_other",
    )(*args)


def fold_kernel(code_ref, parts_ref, out_ref, marked):
    slot = (iota((64, 128), 1) % 32).astype(F32)
    codes = [jnp.broadcast_to(code_ref[:, p : p + 1], (64, 128)) for p in range(8)]
    best = jnp.full((64, 128), NEG, F32)
    for g in range(32):
        rows = parts_ref[4 * g, 32:40, :].astype(F32)
        for r in range(1, 4):
            rows += parts_ref[4 * g + r, 32:40, :].astype(F32)
        m = rows[0:1, :] + rows[1:2, :]
        here = slot + 32.0 * g
        hit = codes[0] == here
        for p in range(1, 8):
            hit = jnp.logical_or(hit, codes[p] == here)
        value = jnp.where(hit, m, NEG)
        marked[g] = value
        best = jnp.maximum(best, value)
    top = jnp.max(best, axis=1, keepdims=True)
    total = jnp.zeros((128, 128), F32)
    for g in range(0, 32, 2):
        pair = []
        for h in range(2):
            w = jnp.exp(marked[g + h] - top)
            first = w.astype(BF)
            pair.append(jnp.concatenate([first, (w - first.astype(F32)).astype(BF)], axis=0))
        weights = jnp.concatenate(pair, axis=1)
        tallies = jnp.concatenate([parts_ref[4 * g + r, 0:32, :] for r in range(8)], axis=0)
        total += jnp.dot(weights, tallies, preferred_element_type=F32)
    votes = total[0:64] + total[64:128]
    out_ref[...] = CLASSES * votes / jnp.sum(votes, axis=1, keepdims=True)


def fold(codes, parts):
    return pl.pallas_call(
        fold_kernel,
        out_shape=jax.ShapeDtypeStruct((64, CLASSES), F32),
        in_specs=[VMEM] * 2,
        out_specs=VMEM,
        scratch_shapes=[pltpu.VMEM((32, 64, 128), F32)],
        compiler_params=grant(8),
        name="fold",
    )(near(codes), near(parts))


def local(queries, bank, labels, probes):
    *chunks, codes = route(queries, probes.T)
    own, other = pick(gather(chunks))
    arrived = lax.ppermute(other, BOTH, [(d, d ^ 4) for d in range(128)])
    mine = score(own, bank, labels)
    blocks = score(arrived, bank, labels, mine)
    parts = lax.all_to_all(
        blocks.reshape(128, ROWS, 128), BOTH, split_axis=0, concat_axis=0, tiled=True
    )
    return fold(codes, parts)


def solution(mesh):
    return jax.shard_map(
        local,
        mesh=mesh,
        in_specs=(
            P(BOTH, None),
            P("dp", "rep", None),
            P("dp", "rep"),
            P(BOTH, None),
        ),
        out_specs=P(BOTH, None),
        check_vma=False,
    )
```

```python
import functools

import jax
import jax.numpy as jnp
from jax import lax
from jax.experimental import pallas as pl
from jax.experimental.pallas import tpu as pltpu
from jax.sharding import PartitionSpec as P

CLASSES = 128
SLOTS = 4
ROWS = 40
NEG = -1.0e30
BOTH = ("dp", "rep")

STRIDE = {"x": 1, "y": 32, "z": 8}
ORDERS = ("xyz", "yzx", "zxy")
BF, F32 = jnp.bfloat16, jnp.float32


def moves(axis, target):
    stride = STRIDE[axis]
    pairs = []
    for d in range(128):
        at = d // stride % 4
        pairs.append((d, d + (target(at) - at) * stride))
    return pairs


def shift(value, axis, step):
    return lax.ppermute(value, BOTH, moves(axis, lambda at: (at + step) % 4))


def swap(value, axis, mask):
    return lax.ppermute(value, BOTH, moves(axis, lambda at: at ^ mask))


def dot_t(a, b):
    return lax.dot_general(a, b, (((1,), (1,)), ((), ())), preferred_element_type=F32)


def near(value):
    return pltpu.with_memory_space_constraint(value, pltpu.VMEM)


def far_off(value):
    return pltpu.with_memory_space_constraint(value, pltpu.HBM)


def grant(mib):
    return pltpu.CompilerParams(vmem_limit_bytes=mib << 20)


VMEM = pl.BlockSpec(memory_space=pltpu.VMEM)
HBM = pl.BlockSpec(memory_space=pltpu.HBM)


def iota(shape, dim):
    return lax.broadcasted_iota(jnp.int32, shape, dim)


def route_kernel(q_ref, probes_ref, c0_ref, c1_ref, c2_ref, code_ref, probes, sems):
    fetch = pltpu.make_async_copy(probes_ref, probes, sems.at[3])
    fetch.start()
    loads = []
    for k, c_ref in enumerate((c0_ref, c1_ref, c2_ref)):
        columns = q_ref.at[:, 256 * k : 256 * k + 256]
        loads.append(pltpu.make_async_copy(columns, c_ref.at[0:64, :], sems.at[k]))
        loads[k].start()
    fetch.wait()
    named = probes[...].astype(F32)
    eye = (iota((64, 64), 0) == iota((64, 64), 1)).astype(BF)
    cols = dot_t(eye, named.astype(BF))
    earlier = iota((64, 64), 0) < iota((64, 64), 1)
    ranks = []
    for p in range(8):
        same = jnp.zeros((64, 64), F32)
        for o in range(8):
            same += (cols[:, o : o + 1] == named[p : p + 1, :]).astype(F32)
        ranks.append(jnp.sum(jnp.where(earlier, same, 0.0), axis=0, keepdims=True))
    rank = jnp.concatenate(ranks, axis=0)
    code_ref[...] = 4.0 * cols + dot_t(eye, rank.astype(BF))
    spread = (iota((64, 128), 0) == iota((64, 128), 1) % 64).astype(BF)
    c0_ref[64:72, 0:128] = jnp.dot(named.astype(BF), spread, preferred_element_type=F32).astype(BF)
    c0_ref[64:72, 128:256] = jnp.dot(rank.astype(BF), spread, preferred_element_type=F32).astype(BF)
    for load in loads:
        load.wait()


def route(queries, probes_t):
    return pl.pallas_call(
        route_kernel,
        out_shape=[pltpu.VMEM((72, 256), BF)]
        + [pltpu.VMEM((64, 256), BF)] * 2
        + [pltpu.VMEM((64, 8), F32)],
        in_specs=[HBM] * 2,
        out_specs=[VMEM] * 4,
        scratch_shapes=[pltpu.VMEM((8, 64), jnp.int32), pltpu.SemaphoreType.DMA((4,))],
        compiler_params=grant(4),
        name="route",
    )(far_off(queries), far_off(probes_t))


def join_kernel(a_ref, b_ref, out_ref):
    size = a_ref.shape[0]
    out_ref[0:size] = a_ref[...]
    out_ref[size : 2 * size] = b_ref[...]


def join(a, b):
    return pl.pallas_call(
        join_kernel,
        out_shape=pltpu.VMEM((2 * a.shape[0],) + a.shape[1:], a.dtype),
        in_specs=[VMEM] * 2,
        out_specs=VMEM,
        compiler_params=grant(4),
        name="join",
    )(near(a), near(b))


def half_kernel(at, a_ref, out_ref):
    out_ref[...] = a_ref[at : at + out_ref.shape[0]]


def half(a, at):
    return pl.pallas_call(
        functools.partial(half_kernel, at),
        out_shape=pltpu.VMEM((a.shape[0] // 2,) + a.shape[1:], a.dtype),
        in_specs=[VMEM],
        out_specs=VMEM,
        compiler_params=grant(4),
        name="half",
    )(near(a))


def gather(chunks):
    held = [c[None] for c in chunks]
    for stage in range(2):
        axes = [ORDERS[k][stage] for k in range(3)]
        for mask in (1, 3):
            other = [swap(held[k], axes[k], mask) for k in range(3)]
            for k in range(3):
                held[k] = join(held[k], other[k])
    axes = [ORDERS[k][2] for k in range(3)]
    up = [shift(held[k], axes[k], -1) for k in range(3)]
    down = [shift(held[k], axes[k], 1) for k in range(3)]
    half_a, half_b = [], []
    for k in range(3):
        half_a.append(half(up[k], 0))
        half_b.append(half(down[k], 8))
    far_a = [shift(half_a[k], axes[k], -1) for k in range(3)]
    far_b = [shift(half_b[k], axes[k], 1) for k in range(3)]
    return [(held[k], up[k], far_a[k], far_b[k], down[k]) for k in range(3)]


def position():
    dp, x = lax.axis_index("dp"), lax.axis_index("rep")
    return dp, (x, dp // 8, dp // 2 % 4), dp % 2


def pick_kernel(*refs):
    dp, here, _ = position()
    coords = [[(me + r) % 4 for r in range(4)] for me in here]
    apart = [[at ^ me for at in ats] for ats, me in zip(coords, here)]
    place = [[d ^ (d >> 1) for d in ds] for ds in apart]
    pieces = [refs[5 * k : 5 * k + 5] for k in range(3)]
    own_ref, other_ref, *far = refs[15:]
    for k in range(3):
        far[k][0:8] = pieces[k][2][...]
        far[k][8:16] = pieces[k][3][...]
    lane = iota((16, 256), 1) // 64
    row = iota((16, 256), 0)
    source = jnp.where(
        lane == 0,
        coords[0][0],
        jnp.where(lane == 1, coords[0][1], jnp.where(lane == 2, coords[0][2], coords[0][3])),
    )
    want = jnp.where(row // 4 == source, row % 4 + 1, -1).astype(F32)
    part = iota((8, 128), 1) // 64
    cluster = iota((8, 256), 0)
    bases = [(dp * 8 + cluster).astype(F32), ((dp ^ 1) * 8 + cluster).astype(F32)]

    def block(k, rx, ry, rz, aux):
        r = (rx, ry, rz)
        order = ["xyz".index(a) for a in ORDERS[k]]
        at = place[order[1]][r[order[1]]] * 4 + place[order[0]][r[order[0]]]
        last = r[order[2]]
        rows = slice(64, 72) if aux else slice(0, 64)
        if last == 2:
            return far[k][at, rows, :]
        return pieces[k][{0: 0, 1: 1, 3: 4}[last]][at, rows, :]

    def pair(a, b):
        return jnp.where(part < 1, a, b)

    def aux_of(blocks, columns):
        a = [b[:, columns] for b in blocks]
        return jnp.concatenate([pair(a[0], a[1]), pair(a[2], a[3])], axis=1)

    for ry in range(4):
        for rz in range(4):
            blocks = [block(0, rx, ry, rz, True).astype(F32) for rx in range(4)]
            probe = aux_of(blocks, slice(0, 128))
            rank = aux_of(blocks, slice(128, 256))
            picks = []
            for g in range(2):
                slot = jnp.zeros((8, 256), F32)
                for p in range(8):
                    slot += jnp.where(probe[p : p + 1, :] == bases[g], rank[p : p + 1, :] + 1.0, 0.0)
                for c in range(8):
                    picks.append(jnp.where(slot[c : c + 1, :] == want, 2.0, 0.0).astype(BF))
            pick = jnp.concatenate(picks, axis=0)
            base = pl.multiple_of((coords[1][ry] * 4 + coords[2][rz]) * 16, 16)
            for k in range(3):
                rows = jnp.concatenate([block(k, rx, ry, rz, False) for rx in range(4)], axis=0)
                found = jnp.dot(pick, rows, preferred_element_type=F32).astype(BF)
                for c in range(8):
                    own_ref[c, pl.ds(base, 16), 256 * k : 256 * k + 256] = found[16 * c : 16 * c + 16]
                    other_ref[c, pl.ds(base, 16), 256 * k : 256 * k + 256] = found[
                        128 + 16 * c : 144 + 16 * c
                    ]


def pick(pieces):
    flat = [near(a) for p in pieces for a in p]
    out = pltpu.VMEM((8, 256, 768), BF)
    return pl.pallas_call(
        pick_kernel,
        out_shape=(out, out),
        in_specs=[VMEM] * 15,
        out_specs=(VMEM, VMEM),
        scratch_shapes=[pltpu.VMEM((16,) + p[0].shape[1:], BF) for p in pieces],
        compiler_params=grant(12),
        name="pick",
    )(*flat)


def score_body(p_ref, bank_ref, labels_ref, acc, tal, wide, shifts, even, odd):
    clusters = p_ref.shape[0]
    lane = iota((64, 128), 1) - lax.axis_index("rep") * 32
    shifts[...] = jnp.zeros_like(shifts)

    def begin(c, held):
        tops = []
        for rows in (slice(r, r + 256) for r in range(0, 1024, 256)):
            s = dot_t(bank_ref[c, rows, :], p_ref[c])
            held[rows, :] = s
            tops.append(jnp.max(s, axis=0, keepdims=True))
        return jnp.maximum(jnp.maximum(tops[0], tops[1]), jnp.maximum(tops[2], tops[3]))

    def finish(c, held, top):
        high = top.astype(BF).astype(F32)
        m = high + (top - high).astype(BF).astype(F32)
        e = jnp.exp(held[...] - m).astype(BF)
        onehot = (labels_ref[pl.ds(c, 1), :] == iota((CLASSES, 1024), 0)).astype(F32).astype(BF)
        tal[...] = jnp.dot(onehot, e, preferred_element_type=F32).T
        wide[...] = jnp.broadcast_to(m, (128, 256)).T
        for j in range(SLOTS):
            acc[pl.ds(c * SLOTS + j, 64, stride=ROWS), :] = tal[pl.ds(j, 64, stride=SLOTS), :]
            shifts[...] = jnp.where(
                lane == c * SLOTS + j, wide[pl.ds(j, 64, stride=SLOTS), :], shifts[...]
            )

    def two(n, top):
        c = 2 * n
        other = begin(c + 1, odd)
        finish(c, even, top)
        top = begin(c + 2, even)
        finish(c + 1, odd, other)
        return top

    top = begin(0, even)
    for n in range(clusters // 2 - 1):
        top = two(n, top)
    other = begin(clusters - 1, odd)
    finish(clusters - 2, even, top)
    finish(clusters - 1, odd, other)
    full = shifts[...]
    first = full.astype(BF).astype(F32)
    acc[pl.ds(32, 64, stride=ROWS), :] = first
    acc[pl.ds(33, 64, stride=ROWS), :] = full - first
    for j in range(34, ROWS):
        acc[pl.ds(j, 64, stride=ROWS), :] = jnp.zeros((64, 128), F32)


def score_own_kernel(p_ref, bank_ref, labels_ref, out_ref, *scratch):
    score_body(p_ref, bank_ref, labels_ref, *scratch)
    out_ref[...] = scratch[0][...].astype(BF)


def score_other_kernel(p_ref, bank_ref, labels_ref, own_ref, out_ref, *scratch):
    score_body(p_ref, bank_ref, labels_ref, *scratch)
    acc, core = scratch[0], position()[2]
    size = 4 * ROWS
    for yz in range(16):
        mine = pl.multiple_of((yz * 2 + core) * size, 16)
        theirs = pl.multiple_of((yz * 2 + 1 - core) * size, 16)
        out_ref[pl.ds(mine, size), :] = own_ref[yz * size : yz * size + size, :]
        out_ref[pl.ds(theirs, size), :] = acc[yz * size : yz * size + size, :].astype(BF)


def score(picked, bank, labels, own=None):
    clusters, rows, width = bank.shape
    count = picked.shape[1]
    args = [near(picked), near(bank), near(labels)]
    out_rows = 64 * ROWS
    if own is not None:
        args.append(near(own))
        out_rows = 128 * ROWS
    return pl.pallas_call(
        score_own_kernel if own is None else score_other_kernel,
        out_shape=pltpu.VMEM((out_rows, 128), BF),
        in_specs=[VMEM] * len(args),
        out_specs=VMEM,
        scratch_shapes=[
            pltpu.VMEM((64 * ROWS, 128), F32),
            pltpu.VMEM((256, 128), F32),
            pltpu.VMEM((256, 128), F32),
            pltpu.VMEM((64, 128), F32),
            pltpu.VMEM((1024, 256), F32),
            pltpu.VMEM((1024, 256), F32),
        ],
        compiler_params=grant(12),
        cost_estimate=pl.CostEstimate(
            flops=2 * clusters * count * rows * (width + 128),
            transcendentals=clusters * count * rows,
            bytes_accessed=bank.size * 2,
        ),
        name="score_own" if own is None else "score_other",
    )(*args)


def marks_kernel(code_ref, marks_ref):
    slot = (iota((64, 128), 1) % 32).astype(F32)
    codes = [jnp.broadcast_to(code_ref[:, p : p + 1], (64, 128)) for p in range(8)]
    for g in range(32):
        here = slot + 32.0 * g
        hit = codes[0] == here
        for p in range(1, 8):
            hit = jnp.logical_or(hit, codes[p] == here)
        marks_ref[g] = jnp.where(hit, 0.0, NEG)


def marks_of(codes):
    return pl.pallas_call(
        marks_kernel,
        out_shape=pltpu.VMEM((32, 64, 128), F32),
        in_specs=[VMEM],
        out_specs=VMEM,
        compiler_params=grant(4),
        name="marks",
    )(near(codes))


def fold_kernel(marks_ref, parts_ref, out_ref, marked):
    best = jnp.full((64, 128), NEG, F32)
    for g in range(32):
        rows = parts_ref[4 * g, 32:40, :].astype(F32)
        for r in range(1, 4):
            rows += parts_ref[4 * g + r, 32:40, :].astype(F32)
        m = rows[0:1, :] + rows[1:2, :]
        value = marks_ref[g] + m
        marked[g] = value
        best = jnp.maximum(best, value)
    top = jnp.max(best, axis=1, keepdims=True)
    total = jnp.zeros((128, 128), F32)
    for g in range(0, 32, 2):
        pair = []
        for h in range(2):
            w = jnp.exp(marked[g + h] - top)
            first = w.astype(BF)
            pair.append(jnp.concatenate([first, (w - first.astype(F32)).astype(BF)], axis=0))
        weights = jnp.concatenate(pair, axis=1)
        tallies = jnp.concatenate([parts_ref[4 * g + r, 0:32, :] for r in range(8)], axis=0)
        total += jnp.dot(weights, tallies, preferred_element_type=F32)
    votes = total[0:64] + total[64:128]
    out_ref[...] = CLASSES * votes / jnp.sum(votes, axis=1, keepdims=True)


def fold(marks, parts):
    return pl.pallas_call(
        fold_kernel,
        out_shape=jax.ShapeDtypeStruct((64, CLASSES), F32),
        in_specs=[VMEM] * 2,
        out_specs=VMEM,
        scratch_shapes=[pltpu.VMEM((32, 64, 128), F32)],
        compiler_params=grant(8),
        name="fold",
    )(near(marks), near(parts))


def local(queries, bank, labels, probes):
    *chunks, codes = route(queries, probes.T)
    pieces = gather(chunks)
    marks = marks_of(codes)
    own, other = pick(pieces)
    arrived = lax.ppermute(other, BOTH, [(d, d ^ 4) for d in range(128)])
    mine = score(own, bank, labels)
    blocks = score(arrived, bank, labels, mine)
    parts = lax.all_to_all(
        blocks.reshape(128, ROWS, 128), BOTH, split_axis=0, concat_axis=0, tiled=True
    )
    return fold(marks, parts)


def solution(mesh):
    return jax.shard_map(
        local,
        mesh=mesh,
        in_specs=(
            P(BOTH, None),
            P("dp", "rep", None),
            P("dp", "rep"),
            P(BOTH, None),
        ),
        out_specs=P(BOTH, None),
        check_vma=False,
    )
```

```python
import functools

import jax
import jax.numpy as jnp
from jax import lax
from jax.experimental import pallas as pl
from jax.experimental.pallas import tpu as pltpu
from jax.sharding import PartitionSpec as P

CLASSES = 128
SLOTS = 4
ROWS = 40
NEG = -1.0e30
BOTH = ("dp", "rep")

STRIDE = {"x": 1, "y": 32, "z": 8}
ORDERS = ("xyz", "yzx", "zxy")
BF, F32 = jnp.bfloat16, jnp.float32


def moves(axis, target):
    stride = STRIDE[axis]
    pairs = []
    for d in range(128):
        at = d // stride % 4
        pairs.append((d, d + (target(at) - at) * stride))
    return pairs


def shift(value, axis, step):
    return lax.ppermute(value, BOTH, moves(axis, lambda at: (at + step) % 4))


def swap(value, axis, mask):
    return lax.ppermute(value, BOTH, moves(axis, lambda at: at ^ mask))


def dot_t(a, b):
    return lax.dot_general(a, b, (((1,), (1,)), ((), ())), preferred_element_type=F32)


def near(value):
    return pltpu.with_memory_space_constraint(value, pltpu.VMEM)


def far_off(value):
    return pltpu.with_memory_space_constraint(value, pltpu.HBM)


def grant(mib):
    return pltpu.CompilerParams(vmem_limit_bytes=mib << 20)


VMEM = pl.BlockSpec(memory_space=pltpu.VMEM)
HBM = pl.BlockSpec(memory_space=pltpu.HBM)


def iota(shape, dim):
    return lax.broadcasted_iota(jnp.int32, shape, dim)


def route_kernel(q_ref, probes_ref, c0_ref, c1_ref, c2_ref, code_ref, probes, sems):
    fetch = pltpu.make_async_copy(probes_ref, probes, sems.at[3])
    fetch.start()
    loads = []
    for k, c_ref in enumerate((c0_ref, c1_ref, c2_ref)):
        columns = q_ref.at[:, 256 * k : 256 * k + 256]
        loads.append(pltpu.make_async_copy(columns, c_ref.at[0:64, :], sems.at[k]))
        loads[k].start()
    fetch.wait()
    named = probes[...].astype(F32)
    eye = (iota((64, 64), 0) == iota((64, 64), 1)).astype(BF)
    cols = dot_t(eye, named.astype(BF))
    earlier = iota((64, 64), 0) < iota((64, 64), 1)
    ranks = []
    for p in range(8):
        same = jnp.zeros((64, 64), F32)
        for o in range(8):
            same += (cols[:, o : o + 1] == named[p : p + 1, :]).astype(F32)
        ranks.append(jnp.sum(jnp.where(earlier, same, 0.0), axis=0, keepdims=True))
    rank = jnp.concatenate(ranks, axis=0)
    code_ref[0:8, :] = named
    code_ref[8:16, :] = rank
    spread = (iota((64, 128), 0) == iota((64, 128), 1) % 64).astype(BF)
    c0_ref[64:72, 0:128] = jnp.dot(named.astype(BF), spread, preferred_element_type=F32).astype(BF)
    c0_ref[64:72, 128:256] = jnp.dot(rank.astype(BF), spread, preferred_element_type=F32).astype(BF)
    for load in loads:
        load.wait()


def route(queries, probes_t):
    return pl.pallas_call(
        route_kernel,
        out_shape=[pltpu.VMEM((72, 256), BF)]
        + [pltpu.VMEM((64, 256), BF)] * 2
        + [pltpu.VMEM((16, 64), F32)],
        in_specs=[HBM] * 2,
        out_specs=[VMEM] * 4,
        scratch_shapes=[pltpu.VMEM((8, 64), jnp.int32), pltpu.SemaphoreType.DMA((4,))],
        compiler_params=grant(4),
        name="route",
    )(far_off(queries), far_off(probes_t))


def join_kernel(a_ref, b_ref, out_ref):
    size = a_ref.shape[0]
    out_ref[0:size] = a_ref[...]
    out_ref[size : 2 * size] = b_ref[...]


def join(a, b):
    return pl.pallas_call(
        join_kernel,
        out_shape=pltpu.VMEM((2 * a.shape[0],) + a.shape[1:], a.dtype),
        in_specs=[VMEM] * 2,
        out_specs=VMEM,
        compiler_params=grant(4),
        name="join",
    )(near(a), near(b))


def half_kernel(at, a_ref, out_ref):
    out_ref[...] = a_ref[at : at + out_ref.shape[0]]


def half(a, at):
    return pl.pallas_call(
        functools.partial(half_kernel, at),
        out_shape=pltpu.VMEM((a.shape[0] // 2,) + a.shape[1:], a.dtype),
        in_specs=[VMEM],
        out_specs=VMEM,
        compiler_params=grant(4),
        name="half",
    )(near(a))


def gather(chunks):
    held = [c[None] for c in chunks]
    for stage in range(2):
        axes = [ORDERS[k][stage] for k in range(3)]
        for mask in (1, 3):
            other = [swap(held[k], axes[k], mask) for k in range(3)]
            for k in range(3):
                held[k] = join(held[k], other[k])
    axes = [ORDERS[k][2] for k in range(3)]
    up = [shift(held[k], axes[k], -1) for k in range(3)]
    down = [shift(held[k], axes[k], 1) for k in range(3)]
    half_a, half_b = [], []
    for k in range(3):
        half_a.append(half(up[k], 0))
        half_b.append(half(down[k], 8))
    far_a = [shift(half_a[k], axes[k], -1) for k in range(3)]
    far_b = [shift(half_b[k], axes[k], 1) for k in range(3)]
    return [(held[k], up[k], far_a[k], far_b[k], down[k]) for k in range(3)]


def position():
    dp, x = lax.axis_index("dp"), lax.axis_index("rep")
    return dp, (x, dp // 8, dp // 2 % 4), dp % 2


def pick_kernel(*refs):
    dp, here, _ = position()
    coords = [[(me + r) % 4 for r in range(4)] for me in here]
    apart = [[at ^ me for at in ats] for ats, me in zip(coords, here)]
    place = [[d ^ (d >> 1) for d in ds] for ds in apart]
    pieces = [refs[5 * k : 5 * k + 5] for k in range(3)]
    own_ref, other_ref, *far = refs[15:]
    for k in range(3):
        far[k][0:8] = pieces[k][2][...]
        far[k][8:16] = pieces[k][3][...]
    lane = iota((16, 256), 1) // 64
    row = iota((16, 256), 0)
    source = jnp.where(
        lane == 0,
        coords[0][0],
        jnp.where(lane == 1, coords[0][1], jnp.where(lane == 2, coords[0][2], coords[0][3])),
    )
    want = jnp.where(row // 4 == source, row % 4 + 1, -1).astype(F32)
    part = iota((8, 128), 1) // 64
    cluster = iota((8, 256), 0)
    bases = [(dp * 8 + cluster).astype(F32), ((dp ^ 1) * 8 + cluster).astype(F32)]

    def block(k, rx, ry, rz, aux):
        r = (rx, ry, rz)
        order = ["xyz".index(a) for a in ORDERS[k]]
        at = place[order[1]][r[order[1]]] * 4 + place[order[0]][r[order[0]]]
        last = r[order[2]]
        rows = slice(64, 72) if aux else slice(0, 64)
        if last == 2:
            return far[k][at, rows, :]
        return pieces[k][{0: 0, 1: 1, 3: 4}[last]][at, rows, :]

    def pair(a, b):
        return jnp.where(part < 1, a, b)

    def aux_of(blocks, columns):
        a = [b[:, columns] for b in blocks]
        return jnp.concatenate([pair(a[0], a[1]), pair(a[2], a[3])], axis=1)

    for ry in range(4):
        for rz in range(4):
            blocks = [block(0, rx, ry, rz, True).astype(F32) for rx in range(4)]
            probe = aux_of(blocks, slice(0, 128))
            rank = aux_of(blocks, slice(128, 256))
            picks = []
            for g in range(2):
                slot = jnp.zeros((8, 256), F32)
                for p in range(8):
                    slot += jnp.where(probe[p : p + 1, :] == bases[g], rank[p : p + 1, :] + 1.0, 0.0)
                for c in range(8):
                    picks.append(jnp.where(slot[c : c + 1, :] == want, 2.0, 0.0).astype(BF))
            pick = jnp.concatenate(picks, axis=0)
            base = pl.multiple_of((coords[1][ry] * 4 + coords[2][rz]) * 16, 16)
            for k in range(3):
                rows = jnp.concatenate([block(k, rx, ry, rz, False) for rx in range(4)], axis=0)
                found = jnp.dot(pick, rows, preferred_element_type=F32).astype(BF)
                for c in range(8):
                    own_ref[c, pl.ds(base, 16), 256 * k : 256 * k + 256] = found[16 * c : 16 * c + 16]
                    other_ref[c, pl.ds(base, 16), 256 * k : 256 * k + 256] = found[
                        128 + 16 * c : 144 + 16 * c
                    ]


def pick(pieces):
    flat = [near(a) for p in pieces for a in p]
    out = pltpu.VMEM((8, 256, 768), BF)
    return pl.pallas_call(
        pick_kernel,
        out_shape=(out, out),
        in_specs=[VMEM] * 15,
        out_specs=(VMEM, VMEM),
        scratch_shapes=[pltpu.VMEM((16,) + p[0].shape[1:], BF) for p in pieces],
        compiler_params=grant(12),
        name="pick",
    )(*flat)


def score_body(p_ref, bank_ref, labels_ref, acc, tal, wide, shifts, even, odd):
    clusters = p_ref.shape[0]
    lane = iota((64, 128), 1) - lax.axis_index("rep") * 32
    shifts[...] = jnp.zeros_like(shifts)

    def begin(c, held):
        tops = []
        for rows in (slice(r, r + 256) for r in range(0, 1024, 256)):
            s = dot_t(bank_ref[c, rows, :], p_ref[c])
            held[rows, :] = s
            tops.append(jnp.max(s, axis=0, keepdims=True))
        return jnp.maximum(jnp.maximum(tops[0], tops[1]), jnp.maximum(tops[2], tops[3]))

    def finish(c, held, top):
        high = top.astype(BF).astype(F32)
        m = high + (top - high).astype(BF).astype(F32)
        e = jnp.exp(held[...] - m).astype(BF)
        onehot = (labels_ref[pl.ds(c, 1), :] == iota((CLASSES, 1024), 0)).astype(F32).astype(BF)
        tal[...] = jnp.dot(onehot, e, preferred_element_type=F32).T
        wide[...] = jnp.broadcast_to(m, (128, 256)).T
        for j in range(SLOTS):
            acc[pl.ds(c * SLOTS + j, 64, stride=ROWS), :] = tal[pl.ds(j, 64, stride=SLOTS), :]
            shifts[...] = jnp.where(
                lane == c * SLOTS + j, wide[pl.ds(j, 64, stride=SLOTS), :], shifts[...]
            )

    def two(n, top):
        c = 2 * n
        other = begin(c + 1, odd)
        finish(c, even, top)
        top = begin(c + 2, even)
        finish(c + 1, odd, other)
        return top

    top = begin(0, even)
    for n in range(clusters // 2 - 1):
        top = two(n, top)
    other = begin(clusters - 1, odd)
    finish(clusters - 2, even, top)
    finish(clusters - 1, odd, other)
    full = shifts[...]
    first = full.astype(BF).astype(F32)
    acc[pl.ds(32, 64, stride=ROWS), :] = first
    acc[pl.ds(33, 64, stride=ROWS), :] = full - first
    for j in range(34, ROWS):
        acc[pl.ds(j, 64, stride=ROWS), :] = jnp.zeros((64, 128), F32)


def score_own_kernel(p_ref, bank_ref, labels_ref, out_ref, *scratch):
    score_body(p_ref, bank_ref, labels_ref, *scratch)
    out_ref[...] = scratch[0][...].astype(BF)


def score_other_kernel(p_ref, bank_ref, labels_ref, own_ref, out_ref, *scratch):
    score_body(p_ref, bank_ref, labels_ref, *scratch)
    acc, core = scratch[0], position()[2]
    size = 4 * ROWS
    for yz in range(16):
        mine = pl.multiple_of((yz * 2 + core) * size, 16)
        theirs = pl.multiple_of((yz * 2 + 1 - core) * size, 16)
        out_ref[pl.ds(mine, size), :] = own_ref[yz * size : yz * size + size, :]
        out_ref[pl.ds(theirs, size), :] = acc[yz * size : yz * size + size, :].astype(BF)


def score(picked, bank, labels, own=None):
    clusters, rows, width = bank.shape
    count = picked.shape[1]
    args = [near(picked), near(bank), near(labels)]
    out_rows = 64 * ROWS
    if own is not None:
        args.append(near(own))
        out_rows = 128 * ROWS
    return pl.pallas_call(
        score_own_kernel if own is None else score_other_kernel,
        out_shape=pltpu.VMEM((out_rows, 128), BF),
        in_specs=[VMEM] * len(args),
        out_specs=VMEM,
        scratch_shapes=[
            pltpu.VMEM((64 * ROWS, 128), F32),
            pltpu.VMEM((256, 128), F32),
            pltpu.VMEM((256, 128), F32),
            pltpu.VMEM((64, 128), F32),
            pltpu.VMEM((1024, 256), F32),
            pltpu.VMEM((1024, 256), F32),
        ],
        compiler_params=grant(12),
        cost_estimate=pl.CostEstimate(
            flops=2 * clusters * count * rows * (width + 128),
            transcendentals=clusters * count * rows,
            bytes_accessed=bank.size * 2,
        ),
        name="score_own" if own is None else "score_other",
    )(*args)


def marks_kernel(code_ref, marks_ref):
    slot = (iota((64, 128), 1) % 32).astype(F32)
    eye = (iota((64, 64), 0) == iota((64, 64), 1)).astype(BF)
    both = dot_t(eye, code_ref[...].astype(BF))
    code = 4.0 * both[:, 0:8] + both[:, 8:16]
    codes = [jnp.broadcast_to(code[:, p : p + 1], (64, 128)) for p in range(8)]
    for g in range(32):
        here = slot + 32.0 * g
        hit = codes[0] == here
        for p in range(1, 8):
            hit = jnp.logical_or(hit, codes[p] == here)
        marks_ref[g] = jnp.where(hit, 0.0, NEG)


def marks_of(codes):
    return pl.pallas_call(
        marks_kernel,
        out_shape=pltpu.VMEM((32, 64, 128), F32),
        in_specs=[VMEM],
        out_specs=VMEM,
        compiler_params=grant(4),
        name="marks",
    )(near(codes))


def fold_kernel(marks_ref, parts_ref, out_ref, marked):
    best = jnp.full((64, 128), NEG, F32)
    for g in range(32):
        rows = parts_ref[4 * g, 32:40, :].astype(F32)
        for r in range(1, 4):
            rows += parts_ref[4 * g + r, 32:40, :].astype(F32)
        m = rows[0:1, :] + rows[1:2, :]
        value = marks_ref[g] + m
        marked[g] = value
        best = jnp.maximum(best, value)
    top = jnp.max(best, axis=1, keepdims=True)
    total = jnp.zeros((128, 128), F32)
    for g in range(0, 32, 2):
        pair = []
        for h in range(2):
            w = jnp.exp(marked[g + h] - top)
            first = w.astype(BF)
            pair.append(jnp.concatenate([first, (w - first.astype(F32)).astype(BF)], axis=0))
        weights = jnp.concatenate(pair, axis=1)
        tallies = jnp.concatenate([parts_ref[4 * g + r, 0:32, :] for r in range(8)], axis=0)
        total += jnp.dot(weights, tallies, preferred_element_type=F32)
    votes = total[0:64] + total[64:128]
    out_ref[...] = CLASSES * votes / jnp.sum(votes, axis=1, keepdims=True)


def fold(marks, parts):
    return pl.pallas_call(
        fold_kernel,
        out_shape=jax.ShapeDtypeStruct((64, CLASSES), F32),
        in_specs=[VMEM] * 2,
        out_specs=VMEM,
        scratch_shapes=[pltpu.VMEM((32, 64, 128), F32)],
        compiler_params=grant(8),
        name="fold",
    )(near(marks), near(parts))


def local(queries, bank, labels, probes):
    *chunks, codes = route(queries, probes.T)
    pieces = gather(chunks)
    marks = marks_of(codes)
    own, other = pick(pieces)
    arrived = lax.ppermute(other, BOTH, [(d, d ^ 4) for d in range(128)])
    mine = score(own, bank, labels)
    blocks = score(arrived, bank, labels, mine)
    parts = lax.all_to_all(
        blocks.reshape(128, ROWS, 128), BOTH, split_axis=0, concat_axis=0, tiled=True
    )
    return fold(marks, parts)


def solution(mesh):
    return jax.shard_map(
        local,
        mesh=mesh,
        in_specs=(
            P(BOTH, None),
            P("dp", "rep", None),
            P("dp", "rep"),
            P(BOTH, None),
        ),
        out_specs=P(BOTH, None),
        check_vma=False,
    )
```
